32 devices in a mesh: row: 4 (over z), replica: 4 (over y, core), feat: 2 (over x).
Axes of the slice: x: 2, y: 2, z: 4, core: 2. Of those that a mesh axis runs over, the one named last changes fastest.
Arguments:
- features: bfloat16 [4, 4096, 256], P('replica', ('row', 'feat')), may hold values from -6 to 6
- tiles: bfloat16 [4, 32, 4, 3, 128, 128], P('replica', ('row', 'feat')), may hold values from 0 to 1
- block_cols: int32 [4, 32, 4, 3], P('replica', ('row', 'feat')), may hold values from 0 to 7
- block_counts: int32 [4, 32, 4], P('replica', ('row', 'feat')), may hold values from 0 to 3, as said below
- degrees: int32 [4, 4096], P('replica', ('row', 'feat')), may hold values from 32 to 287
- w_self: bfloat16 [256, 256], P(None, 'feat'), may hold values from -0.375 to 0.375
- w_neigh: bfloat16 [256, 256], P(None, 'feat'), may hold values from -0.375 to 0.375
- gamma: float32 [256], P('feat'), may hold values from 0.5 to 1.5
- beta: float32 [256], P('feat'), may hold values from -3 to 3
Outputs:
- hidden_out: bfloat16 [4, 4096, 256], P('replica', 'row', 'feat')
The draws below stay inside these ranges and needn't reach their ends.
Inputs may be any that keep to these rules, and one draw needn't show every extreme that they name: `block_counts`: some block row uses all 3 slots of some source shard in every partition.
All inputs are finite; a program needn't handle non-finite values.
Results may differ from the reference program's by a relative error of at most 0.001.
Values may be sent and summed in bfloat16 or wider, within the bound.
No kernel may reach another device: no remote copies, remote signals or barrier semaphores. Data moves between devices by JAX's collectives and lax.ppermute only.
A program may use at most 128 MiB of HBM per device.

```python
import jax
import jax.numpy as jnp
from jax import lax

F = 256
BLK = 128
CAP = 3
SOURCES = 4
NODES = 4096
NBLK = 32
SHB = 8
PARTS_SIZE = 4


def draw_block_counts(key, part):
    keys = jax.random.split(jax.random.fold_in(key, 11), 4)
    heavy = jax.random.randint(keys[0], (PARTS_SIZE, NBLK, 1), 0, 2)
    upper = jax.random.randint(keys[1], (PARTS_SIZE, NBLK, SOURCES), 1, CAP + 1)
    lower = jax.random.randint(keys[2], (PARTS_SIZE, NBLK, SOURCES), 0, 2)
    counts = jnp.where(heavy == 1, upper, lower).reshape(PARTS_SIZE, NBLK * SOURCES)
    spot = jax.random.randint(keys[3], (PARTS_SIZE, 1), 0, NBLK * SOURCES)
    index = jnp.arange(NBLK * SOURCES, dtype=jnp.int32)[None, :]
    counts = jnp.where(index == spot, CAP, counts)
    return counts.reshape(PARTS_SIZE, NBLK, SOURCES).astype(jnp.int32)


def draw_degrees(key, part):
    base = jax.random.randint(jax.random.fold_in(key, 23), (PARTS_SIZE, NODES), 32, 97)
    index = jnp.arange(NODES, dtype=jnp.int32)[None, :]
    base = jnp.where(index == 0, 32, jnp.where(index == NODES - 1, 96, base))
    return (base * (NODES + 2 * index) // NODES).astype(jnp.int32)


def plant(drawn, rng, smallest, top_value):
    index_at = [jax.random.randint(jax.random.fold_in(rng, axis), (), 0, length) for axis, length in enumerate(drawn.shape)]
    main_axis = drawn.shape.index(max(drawn.shape))
    next_to = index_at[:main_axis] + [(index_at[main_axis] + 1) % drawn.shape[main_axis]] + index_at[main_axis + 1:]
    return drawn.at[tuple(index_at)].set(smallest).at[tuple(next_to)].set(top_value)


def levels(rng, shape, cuts, least, high):
    def one(position, shards_of):
        draws = jax.random.uniform(jax.random.fold_in(jax.random.fold_in(rng, 6), position), (shards_of,), jnp.float32, least / len(cuts), high / len(cuts))
        return jnp.repeat(jnp.exp(draws), shape[position] // shards_of).reshape((-1,) + (1,) * (len(shape) - position - 1))

    level = one(*cuts[0])
    for cut in cuts[1:]:
        level = level * one(*cut)
    return level


def normal_values(stream_key, extent, width, reach, pieces=(), kind=jnp.bfloat16):
    drawn = width * jax.random.normal(stream_key, extent, jnp.float32)
    if pieces:
        drawn = drawn * levels(stream_key, extent, pieces, -0.22, 0.18)
    return jnp.clip(drawn, -reach, reach).astype(kind)


def setup_inputs(seed: int = 0) -> dict:
    seeds = jax.random.split(jax.random.key(seed), 10)
    return {
        "features": normal_values(seeds[0], (PARTS_SIZE, NODES, F), 1.0, 6.0, ((0, 4), (1, 8))),
        "tiles": jnp.clip(1.0 * jax.random.uniform(seeds[1], (PARTS_SIZE, NBLK, SOURCES, CAP, BLK, BLK), jnp.float32) ** levels(seeds[1], (PARTS_SIZE, NBLK, SOURCES, CAP, BLK, BLK), ((0, 4), (1, 8)), -0.2, 0.2), 0.0, 1.0).astype(jnp.bfloat16),
        "block_cols": plant(jax.random.randint(seeds[2], (PARTS_SIZE, NBLK, SOURCES, CAP), 0, SHB), jax.random.fold_in(seeds[2], 1), 0, SHB - 1).astype(jnp.int32),
        "block_counts": draw_block_counts(jax.random.fold_in(seeds[9], 71), 0),
        "degrees": draw_degrees(jax.random.fold_in(seeds[9], 71), 0),
        "w_self": normal_values(seeds[5], (F, F), F ** -0.5, 0.375, ((1, 2),)),
        "w_neigh": normal_values(seeds[6], (F, F), F ** -0.5, 0.375, ((1, 2),)),
        "gamma": jnp.clip(1.0 + 0.1 * jax.random.normal(seeds[7], (F,), jnp.float32), 0.5, 1.5),
        "beta": normal_values(seeds[8], (F,), 0.5, 3.0, ((0, 2),), jnp.float32),
    }


def reference(features, tiles, block_cols, block_counts, degrees, w_self, w_neigh, gamma, beta):
    pres = []
    for part in range(PARTS_SIZE):
        xs = features[part]
        blocks = xs.reshape(NBLK, BLK, F).astype(jnp.float32)
        offsets = (jnp.arange(SOURCES, dtype=jnp.int32) * SHB)[None, :, None]
        glob = (block_cols[part] + offsets).astype(jnp.int32)
        valid = jnp.arange(CAP, dtype=jnp.int32)[None, None, :] < block_counts[part][:, :, None]

        def row_block(args):
            where_cols, used, tile_set = args
            picked = blocks[where_cols]
            masked = jnp.where(used[:, :, None, None], tile_set.astype(jnp.float32), jnp.float32(0.0))
            return jnp.einsum('scij,scjf->if', masked, picked)
        agg_sum = lax.map(row_block, (glob, valid, tiles[part])).reshape(NODES, F)
        agg = (agg_sum / degrees[part][:, None].astype(jnp.float32)).astype(jnp.bfloat16)
        pre = jnp.dot(xs, w_self, preferred_element_type=jnp.float32) + jnp.dot(agg, w_neigh, preferred_element_type=jnp.float32)
        pres.append(pre)
    stacked = jnp.stack(pres)
    mean = lax.optimization_barrier(jnp.mean(stacked, axis=(0, 1)))
    msq = lax.optimization_barrier(jnp.mean(stacked * stacked, axis=(0, 1)))
    var = msq - mean * mean
    normed = gamma * (stacked - mean) / jnp.sqrt(var + 1e-05) + beta
    return jnp.maximum(normed, 0.0).astype(jnp.bfloat16)
```

```python
import functools

import jax
import jax.numpy as jnp
from jax import lax
from jax.experimental import pallas as pl
from jax.experimental.pallas import tpu as pltpu
from jax.sharding import PartitionSpec as P

AXES = ("row", "replica", "feat")
KERNEL_VMEM = 12 * 1024 * 1024


def whole(shape):
    return pl.BlockSpec(shape, lambda *_: (0,) * len(shape))


def place(xs_ref, piece_refs, feat, blocks, block):
    count = len(piece_refs)
    for k, ref in enumerate(piece_refs):
        owner = lax.rem(feat - k + count, count)
        xs_ref[pl.ds(owner * blocks, blocks)] = ref[...].reshape(blocks, block, ref.shape[-1])


def add_shard(acc, tiles_ref, xs_ref, cols_ref, counts_ref, shard, shards):
    row_blocks, _, slots, block, _ = tiles_ref.shape
    out = []
    for b in range(row_blocks):
        used = counts_ref[b, shard]
        left, right = [], []
        for c in range(slots):
            col = cols_ref[c, b, shard]
            tile = tiles_ref[b, 0, c]
            left.append(jnp.where(c < used, tile, jnp.zeros_like(tile)))
            right.append(xs_ref[col])
        part = jnp.dot(
            jnp.concatenate(left, axis=1),
            jnp.concatenate(right, axis=0),
            preferred_element_type=jnp.float32,
        )
        out.append(part if acc is None else acc[b] + part)
    return out


def aggregate_kernel(shards, feats, sources, first, where_ref, cols_ref, counts_ref, *refs):
    refs = list(refs)
    xs_ref = refs.pop()
    acc_out = refs.pop()
    acc_ref = None if first else refs.pop(0)
    row_blocks = acc_out.shape[0]
    acc = None if first else [acc_ref[b] for b in range(row_blocks)]
    feat = where_ref[0]
    for g in range(sources):
        tiles_ref, *pieces = refs[g * (1 + feats):(g + 1) * (1 + feats)]
        block = tiles_ref.shape[-1]
        place(xs_ref.at[g], pieces, feat, xs_ref.shape[1] // feats, block)
        acc = add_shard(acc, tiles_ref, xs_ref.at[g], cols_ref, counts_ref, where_ref[1 + g], shards)
    for b in range(row_blocks):
        acc_out[b] = acc[b]


def finish_kernel(shards, feats, where_ref, cols_ref, counts_ref, acc_ref, tiles_ref, *refs):
    refs = list(refs)
    xs_ref = refs.pop()
    stats_ref = refs.pop()
    pre_refs = refs[-feats:]
    refs = refs[:-feats]
    pieces = refs[:feats]
    own_ref, degrees_ref = refs[feats:feats + 2]
    weights = refs[feats + 2:]
    row_blocks, block = acc_ref.shape[0], acc_ref.shape[1]
    feat = where_ref[0]
    place(xs_ref, pieces, feat, xs_ref.shape[0] // feats, block)
    acc = add_shard([acc_ref[b] for b in range(row_blocks)], tiles_ref, xs_ref, cols_ref, counts_ref, where_ref[1], shards)
    w_self = jnp.concatenate([w[0] for w in weights], axis=1)
    w_neigh = jnp.concatenate([w[1] for w in weights], axis=1)
    width = weights[0].shape[-1]
    total = square = 0.0
    for b in range(row_blocks):
        rows = pl.ds(b * block, block)
        agg = (acc[b] / degrees_ref[rows, :]).astype(jnp.bfloat16)
        pre = jnp.dot(own_ref[rows, :], w_self, preferred_element_type=jnp.float32) + jnp.dot(
            agg, w_neigh, preferred_element_type=jnp.float32
        )
        total += jnp.sum(pre, axis=0, keepdims=True)
        square += jnp.sum(pre * pre, axis=0, keepdims=True)
        for k in range(feats):
            pre_refs[k][rows, :] = pre[:, k * width:(k + 1) * width]
    both = jnp.concatenate([total, square], axis=0)
    for target in range(feats):
        k_here = lax.rem(feat - target + feats, feats)
        chosen = both[:, :width]
        for k in range(1, feats):
            chosen = jnp.where(k_here == k, both[:, k * width:(k + 1) * width], chosen)
        stats_ref[:, target] = jnp.broadcast_to(chosen[None], (stats_ref.shape[0],) + chosen.shape)


def normalize_kernel(total_nodes, feats, where_ref, stats_ref, gamma_ref, beta_ref, *refs):
    out_ref = refs[-1]
    sums = jnp.sum(stats_ref[...], axis=0)
    mean = sums[0:1] / total_nodes
    var = sums[1:2] / total_nodes - mean * mean
    scale = gamma_ref[...] / jnp.sqrt(var + 1e-05)
    rows = refs[0].shape[0]
    for k in range(feats):
        owner = lax.rem(where_ref[0] - k + feats, feats)
        normed = (refs[k][...] - mean) * scale + beta_ref[...]
        out_ref[pl.ds(pl.multiple_of(owner * rows, rows), rows), :] = jnp.maximum(normed, 0.0).astype(out_ref.dtype)


def per_device(shards, feats, replicas, features, tiles, block_cols, block_counts, degrees, w_self, w_neigh, gamma, beta):
    own = features[0]
    local_tiles = tiles[0]
    cols = jnp.transpose(block_cols[0], (2, 0, 1))
    counts = block_counts[0]
    degrees = degrees[0].astype(jnp.float32)[:, None]
    rows, width = own.shape
    row_blocks, _, slots, block, _ = local_tiles.shape
    feat = lax.axis_index("feat")
    row = lax.axis_index("row")
    xor = shards & (shards - 1) == 0

    def to_row(value, k):
        perm = [(i, i ^ k if xor else (i + k) % shards) for i in range(shards)]
        return lax.ppermute(value, "row", perm)

    def to_feat(value, k):
        return lax.ppermute(value, "feat", [(i, (i + k) % feats) for i in range(feats)])

    def source(k):
        return row ^ k if xor else lax.rem(row - k + shards, shards)

    def spread(here):
        return [here] + [to_feat(here, k) for k in range(1, feats)]

    tile_spec = lambda g: pl.BlockSpec(
        (row_blocks, 1, slots, block, block), lambda i, where, cols, counts: (0, where[1 + g], 0, 0, 0)
    )
    acc_shape = (row_blocks, block, width)
    xs_shape = (feats * rows // block, block, width)

    def where_of(ks):
        return jnp.stack([feat] + [source(k) for k in ks]).astype(jnp.int32)

    def aggregate(acc, ks):
        operands = [] if acc is None else [acc]
        specs = [] if acc is None else [whole(acc_shape)]
        for g, k in enumerate(ks):
            operands += [local_tiles] + pieces[k]
            specs += [tile_spec(g)] + [whole((rows, width))] * feats
        return pl.pallas_call(
            functools.partial(aggregate_kernel, shards, feats, len(ks), acc is None),
            out_shape=jax.ShapeDtypeStruct(acc_shape, jnp.float32),
            grid_spec=pltpu.PrefetchScalarGridSpec(
                num_scalar_prefetch=3, grid=(1,), in_specs=specs, out_specs=whole(acc_shape),
                scratch_shapes=[pltpu.VMEM((len(ks),) + xs_shape, own.dtype)],
            ),
            compiler_params=pltpu.CompilerParams(vmem_limit_bytes=KERNEL_VMEM),
            cost_estimate=pl.CostEstimate(
                flops=2 * rows * slots * block * width * len(ks), bytes_accessed=2 * rows * width * 2 * len(ks), transcendentals=0
            ),
        )(places[ks[0]], cols, counts, *operands)

    arrived = [own] + [to_row(own, k) for k in range(1, shards)]
    pieces = [spread(own)]
    weights = spread(jnp.stack([w_self, w_neigh]))
    places = [where_of([k]) for k in range(shards)]
    arrived[1], cols, counts, degrees, places = lax.optimization_barrier((arrived[1], cols, counts, degrees, places))
    pieces.append(spread(arrived[1]))
    acc = aggregate(None, [0])
    if shards > 2:
        arrived[2], acc, weights = lax.optimization_barrier((arrived[2], acc, weights))
    pieces += [spread(here) for here in arrived[2:]]
    for k in range(1, shards - 1):
        acc = aggregate(acc, [k])
    last = shards - 1
    channels = w_self.shape[1]
    groups = shards * replicas
    *pre, stats = pl.pallas_call(
        functools.partial(finish_kernel, shards, feats),
        out_shape=[jax.ShapeDtypeStruct((rows, channels), jnp.float32)] * feats
        + [jax.ShapeDtypeStruct((groups, feats, 2, channels), jnp.float32)],
        grid_spec=pltpu.PrefetchScalarGridSpec(
            num_scalar_prefetch=3,
            grid=(1,),
            in_specs=[whole(acc_shape), tile_spec(0)]
            + [whole((rows, width))] * feats
            + [whole((rows, width)), whole((rows, 1))]
            + [whole((2, width, channels))] * feats,
            out_specs=[whole((rows, channels))] * feats + [whole((groups, feats, 2, channels))],
            scratch_shapes=[pltpu.VMEM(xs_shape, own.dtype)],
        ),
        compiler_params=pltpu.CompilerParams(vmem_limit_bytes=KERNEL_VMEM),
    )(
        places[last], cols, counts, acc, local_tiles, *pieces[last], own,
        degrees, *weights,
    )
    received = [pre[0]] + [to_feat(pre[k], feats - k) for k in range(1, feats)]
    received = [received[0]] + [received[feats - k] for k in range(1, feats)]
    stats = lax.all_to_all(stats.reshape(groups * feats, 2, channels), AXES, 0, 0)
    out = pl.pallas_call(
        functools.partial(normalize_kernel, rows * feats * groups, feats),
        out_shape=jax.ShapeDtypeStruct((rows * feats, channels), jnp.bfloat16),
        grid_spec=pltpu.PrefetchScalarGridSpec(
            num_scalar_prefetch=1,
            grid=(1,),
            in_specs=[whole((groups * feats, 2, channels)), whole((1, channels)), whole((1, channels))]
            + [whole((rows, channels))] * feats,
            out_specs=whole((rows * feats, channels)),
        ),
        compiler_params=pltpu.CompilerParams(vmem_limit_bytes=KERNEL_VMEM),
    )(feat[None].astype(jnp.int32), stats, gamma[None], beta[None], *received)
    return out[None]


def solution(mesh):
    in_specs = (
        P("replica", ("row", "feat"), None),
        P("replica", ("row", "feat"), None, None, None, None),
        P("replica", ("row", "feat"), None, None),
        P("replica", ("row", "feat"), None),
        P("replica", ("row", "feat")),
        P(None, "feat"),
        P(None, "feat"),
        P("feat"),
        P("feat"),
    )
    out_specs = P("replica", "row", "feat")
    body = functools.partial(per_device, mesh.shape["row"], mesh.shape["feat"], mesh.shape["replica"])
    return jax.shard_map(body, mesh=mesh, in_specs=in_specs, out_specs=out_specs, check_vma=False)
```

```python
import functools

import jax
import jax.numpy as jnp
from jax import lax
from jax.experimental import pallas as pl
from jax.experimental.pallas import tpu as pltpu
from jax.sharding import PartitionSpec as P


AXES = ("row", "replica", "feat")
KERNEL_VMEM = 12 * 1024 * 1024


def whole(shape):
    return pl.BlockSpec(shape, lambda *_: (0,) * len(shape))


def place(where_ref, piece_refs, xs_buf, feats):
    blocks = xs_buf.shape[1] // feats
    for g in range(xs_buf.shape[0]):
        for k, ref in enumerate(piece_refs[g * feats:(g + 1) * feats]):
            owner = lax.rem(where_ref[0] - k + feats, feats)
            xs_buf[g, pl.ds(owner * blocks, blocks)] = ref[...]


def block_row(where_ref, tile_refs, xs_buf, shards, ks, b):
    row_blocks, _, slots = tile_refs[0].shape[:3]
    counts_at = 1 + shards
    cols_at = counts_at + row_blocks * shards
    total = None
    for g, k in enumerate(ks):
        shard = where_ref[1 + k]
        used = where_ref[counts_at + b * shards + shard]
        left, right = [], []
        for c in range(slots):
            col = where_ref[cols_at + (c * row_blocks + b) * shards + shard]
            tile = tile_refs[g][b, 0, c]
            left.append(jnp.where(c < used, tile, jnp.zeros_like(tile)))
            right.append(xs_buf[g, col])
        part = jnp.dot(
            jnp.concatenate(left, axis=1),
            jnp.concatenate(right, axis=0),
            preferred_element_type=jnp.float32,
        )
        total = part if total is None else total + part
    return total


def split(refs, count):
    return list(refs[:count]), list(refs[count:])


def aggregate_kernel(shards, feats, ks, first, where_ref, *refs):
    tiles, refs = split(refs, len(ks))
    pieces, refs = split(refs, len(ks) * feats)
    if first:
        degrees_ref, *weights = refs[:1 + feats]
        acc_out, inverse_ref, self_ref, xs_buf = refs[1 + feats:]
        own = pieces[ks.index(0) * feats]
        term = jnp.dot(
            own[...].reshape(-1, own.shape[-1]),
            jnp.concatenate([ref[0] for ref in weights], axis=1),
            preferred_element_type=jnp.float32,
        )
    else:
        acc_ref, acc_out, xs_buf = refs
    place(where_ref, pieces, xs_buf, feats)
    parts = [block_row(where_ref, tiles, xs_buf, shards, ks, b) for b in range(acc_out.shape[0])]
    if first:
        self_ref[...] = term
    for b, part in enumerate(parts):
        if first:
            degree = jnp.broadcast_to(degrees_ref[b:b + 1, :].astype(jnp.float32), inverse_ref.shape[1:])
            inverse_ref[b] = 1.0 / jnp.transpose(degree)
        acc_out[b] = part if first else acc_ref[b] + part


def finish_kernel(shards, feats, ks, where_ref, *refs):
    tiles, refs = split(refs, len(ks))
    pieces, refs = split(refs, len(ks) * feats)
    (acc_ref, inverse_ref, self_ref), refs = split(refs, 3)
    weights, refs = split(refs, feats)
    pre_refs, (stats_ref, xs_buf) = split(refs, feats)
    width = weights[0].shape[-1]
    feat = where_ref[0]
    place(where_ref, pieces, xs_buf, feats)
    row_blocks, block, inner = acc_ref.shape
    agg = []
    for b in range(row_blocks):
        acc = acc_ref[b] + block_row(where_ref, tiles, xs_buf, shards, ks, b)
        agg.append((acc * jnp.concatenate([inverse_ref[b]] * (inner // block), axis=1)).astype(jnp.bfloat16))
    w_neigh = jnp.concatenate([ref[1] for ref in weights], axis=1)
    pre = self_ref[...] + jnp.dot(jnp.concatenate(agg, axis=0), w_neigh, preferred_element_type=jnp.float32)
    total = jnp.sum(pre, axis=0, keepdims=True)
    square = jnp.sum(pre * pre, axis=0, keepdims=True)
    for k in range(feats):
        pre_refs[k][...] = pre[:, k * width:(k + 1) * width]
    both = jnp.concatenate([total, square], axis=0)
    for target in range(feats):
        k_here = lax.rem(feat - target + feats, feats)
        chosen = both[:, :width]
        for k in range(1, feats):
            chosen = jnp.where(k_here == k, both[:, k * width:(k + 1) * width], chosen)
        stats_ref[:, target] = jnp.broadcast_to(chosen[None], (stats_ref.shape[0],) + chosen.shape)


def normalize_kernel(total_nodes, feats, where_ref, stats_ref, gamma_ref, beta_ref, *refs):
    out_ref = refs[-1]
    sums = jnp.sum(stats_ref[...], axis=0)
    mean = sums[0:1] / total_nodes
    var = sums[1:2] / total_nodes - mean * mean
    scale = gamma_ref[...] / jnp.sqrt(var + 1e-05)
    rows = refs[0].shape[0]
    for k in range(feats):
        owner = lax.rem(where_ref[0] - k + feats, feats)
        normed = (refs[k][...] - mean) * scale + beta_ref[...]
        out_ref[pl.ds(pl.multiple_of(owner * rows, rows), rows), :] = jnp.maximum(normed, 0.0).astype(out_ref.dtype)


def ring_of(shards):
    return list(range(0, shards, 2)) + list(range(1, shards, 2))[::-1]


def routes_of(shards):
    routes = {}
    for step in range(1, shards // 2 + 1):
        routes[step] = (step - 1, 1)
        back = shards - step
        if back not in routes:
            routes[back] = ((back + 1) % shards, -1)
    return routes


def per_device(shards, feats, replicas, features, tiles, block_cols, block_counts, degrees, w_self, w_neigh, gamma, beta):
    own = features[0]
    local_tiles = tiles[0]
    rows, width = own.shape
    row_blocks, _, slots, block, _ = local_tiles.shape
    blocks = rows // block
    channels = w_self.shape[1]
    degrees = degrees[0].reshape(blocks, block)
    feat = lax.axis_index("feat")
    row = lax.axis_index("row")
    ring = ring_of(shards)

    def to_row(value, way):
        perm = [(ring[i], ring[(i + way) % shards]) for i in range(shards)]
        return lax.ppermute(value, "row", perm)

    def to_feat(value, k):
        return lax.ppermute(value, "feat", [(i, (i + k) % feats) for i in range(feats)])

    def spread(here):
        return [here] + [to_feat(here, k) for k in range(1, feats)]

    table = [[ring[(ring.index(i) - k) % shards] for k in range(shards)] for i in range(shards)]
    source_rows = lax.dynamic_index_in_dim(jnp.array(table, jnp.int32), row, 0, keepdims=False)
    where = jnp.concatenate(
        [feat[None].astype(jnp.int32), source_rows]
        + [block_counts[0].reshape(-1), jnp.transpose(block_cols[0], (2, 0, 1)).reshape(-1)]
    )
    acc_shape = (row_blocks, block, width)

    piece_shape = (blocks, block, width)

    def sources(ks):
        operands = [local_tiles] * len(ks) + [piece.reshape(piece_shape) for k in ks for piece in pieces[k]]
        specs = [
            pl.BlockSpec((row_blocks, 1, slots, block, block), lambda i, where, k=k: (0, where[1 + k], 0, 0, 0))
            for k in ks
        ]
        specs += [whole(piece_shape)] * (len(ks) * feats)
        return operands, specs, [pltpu.VMEM((len(ks), feats * blocks, block, width), own.dtype)]

    def aggregate(acc, ks):
        operands, specs, scratch = sources(ks)
        first = acc is None
        shapes = [acc_shape]
        if first:
            operands, shapes = operands + [degrees] + weights, shapes + [(blocks, block, block), (rows, feats * channels)]
            specs = specs + [whole((blocks, block))] + [whole((2, width, channels))] * feats
        else:
            operands, specs = operands + [acc], specs + [whole(acc_shape)]
        return pl.pallas_call(
            functools.partial(aggregate_kernel, shards, feats, ks, first),
            out_shape=[jax.ShapeDtypeStruct(shape, jnp.float32) for shape in shapes],
            grid_spec=pltpu.PrefetchScalarGridSpec(
                num_scalar_prefetch=1,
                grid=(1,),
                in_specs=specs,
                out_specs=[whole(shape) for shape in shapes],
                scratch_shapes=scratch,
            ),
            compiler_params=pltpu.CompilerParams(vmem_limit_bytes=KERNEL_VMEM),
            cost_estimate=pl.CostEstimate(
                flops=2 * rows * slots * block * width * len(ks),
                bytes_accessed=2 * rows * width * 2 * len(ks),
                transcendentals=0,
            ),
        )(where, *operands)

    routes = routes_of(shards)
    first, *rest = routes
    last = shards // 2
    arrived, pieces = {0: own}, {0: spread(own)}
    for k, (parent, way) in routes.items():
        if parent == 0:
            arrived[k] = to_row(own, way)
    weights = spread(jnp.stack([w_self, w_neigh]))
    arrived[first], where = lax.optimization_barrier((arrived[first], where))
    for k, (parent, way) in routes.items():
        if k not in arrived:
            arrived[k] = to_row(arrived[parent], way)
        if k != last:
            pieces[k] = spread(arrived[k])
    parent, way = routes[last]
    pieces[last] = [arrived[last]] + [to_row(pieces[parent][k], way) for k in range(1, feats)]
    ends = [last]
    acc, inverse, self_term = aggregate(None, [0] if first == last else [0, first])
    for k in rest:
        if k not in ends:
            (acc,) = aggregate(acc, [k])
    groups = shards * replicas
    operands, specs, scratch = sources(ends)
    *pre, stats = pl.pallas_call(
        functools.partial(finish_kernel, shards, feats, ends),
        out_shape=[jax.ShapeDtypeStruct((rows, channels), jnp.float32)] * feats
        + [jax.ShapeDtypeStruct((groups, feats, 2, channels), jnp.float32)],
        grid_spec=pltpu.PrefetchScalarGridSpec(
            num_scalar_prefetch=1,
            grid=(1,),
            in_specs=specs
            + [whole(acc_shape), whole((blocks, block, block)), whole((rows, feats * channels))]
            + [whole((2, width, channels))] * feats,
            out_specs=[whole((rows, channels))] * feats + [whole((groups, feats, 2, channels))],
            scratch_shapes=scratch,
        ),
        compiler_params=pltpu.CompilerParams(vmem_limit_bytes=KERNEL_VMEM),
    )(where, *operands, acc, inverse, self_term, *weights)
    received = [pre[0]] + [to_feat(pre[k], feats - k) for k in range(1, feats)]
    received = [received[0]] + [received[feats - k] for k in range(1, feats)]
    stats = lax.all_to_all(stats.reshape(groups * feats, 2, channels), AXES, 0, 0)
    out = pl.pallas_call(
        functools.partial(normalize_kernel, rows * feats * groups, feats),
        out_shape=jax.ShapeDtypeStruct((rows * feats, channels), jnp.bfloat16),
        grid_spec=pltpu.PrefetchScalarGridSpec(
            num_scalar_prefetch=1,
            grid=(1,),
            in_specs=[whole((groups * feats, 2, channels)), whole((1, channels)), whole((1, channels))]
            + [whole((rows, channels))] * feats,
            out_specs=whole((rows * feats, channels)),
        ),
        compiler_params=pltpu.CompilerParams(vmem_limit_bytes=KERNEL_VMEM),
    )(feat[None].astype(jnp.int32), stats, gamma[None], beta[None], *received)
    return out[None]


def solution(mesh):
    in_specs = (
        P("replica", ("row", "feat"), None),
        P("replica", ("row", "feat"), None, None, None, None),
        P("replica", ("row", "feat"), None, None),
        P("replica", ("row", "feat"), None),
        P("replica", ("row", "feat")),
        P(None, "feat"),
        P(None, "feat"),
        P("feat"),
        P("feat"),
    )
    out_specs = P("replica", "row", "feat")
    shards, feats = mesh.shape["row"], mesh.shape["feat"]

    def body(*args):
        return per_device(shards, feats, mesh.shape["replica"], *args)

    return jax.shard_map(body, mesh=mesh, in_specs=in_specs, out_specs=out_specs, check_vma=False)
```
